32 devices in a mesh: batch: 2 (over x), ctx: 4 (over y, core), mp: 4 (over z).
Axes of the slice: x: 2, y: 2, z: 4, core: 2. Of those that a mesh axis runs over, the one named last changes fastest.
Arguments:
- hidden_in: bfloat16 [4, 512, 1024], P('batch', 'ctx'), may hold values from -6 to 6
- segment_ids: int32 [4, 512], P('batch', 'ctx'), may hold values from 0 to 3, never falling along the last dimension, each value on 1 to 256 neighbouring positions
- gains: bfloat16 [2, 2, 1024], P(None, None, ('batch', 'ctx', 'mp')), may hold values from 0.5 to 1.5
- biases: bfloat16 [2, 10, 1024], P(None, None, ('batch', 'ctx', 'mp')), may hold values from -3 to 3
- w_qkv: bfloat16 [2, 1024, 3, 1024], P(None, ('batch', 'ctx'), None, 'mp'), may hold values from -0.1875 to 0.1875
- w_out_t: bfloat16 [2, 1024, 1024], P(None, ('batch', 'ctx'), 'mp'), may hold values from -0.5 to 0.5
- w_up: bfloat16 [2, 1024, 4096], P(None, ('batch', 'ctx'), 'mp'), may hold values from -0.1875 to 0.1875
- w_down_t: bfloat16 [2, 1024, 4096], P(None, ('batch', 'ctx'), 'mp'), may hold values from -0.09375 to 0.09375
- grad_out: bfloat16 [4, 512, 1024], P('batch', 'ctx'), may hold values from -6 to 6
Outputs:
- output: bfloat16 [4, 512, 1024], P('batch', 'ctx')
- grad_in: bfloat16 [4, 512, 1024], P('batch', 'ctx')
- grad_gains: float32 [2, 2, 1024], P(None, None, ('batch', 'ctx', 'mp'))
- grad_biases: float32 [2, 10, 1024], P(None, None, ('batch', 'ctx', 'mp'))
- grad_qkv: float32 [2, 1024, 3, 1024], P(None, ('batch', 'ctx'), None, 'mp')
- grad_attn_out: float32 [2, 1024, 1024], P(None, ('batch', 'ctx'), 'mp')
- grad_up: float32 [2, 1024, 4096], P(None, ('batch', 'ctx'), 'mp')
- grad_down: float32 [2, 1024, 4096], P(None, ('batch', 'ctx'), 'mp')
The draws below stay inside these ranges and needn't reach their ends.
Inputs may be any that keep to these rules, and one draw needn't show every extreme that they name: `segment_ids`: document numbers never fall along a sequence; every document spans 1 to 256 tokens, and one of each sequence spans exactly that many.
All inputs are finite; a program needn't handle non-finite values.
Results may differ from the reference program's by a relative error of at most 0.023.
Values may be sent and summed in bfloat16 or wider, within the bound.
A program may use at most 128 MiB of HBM per device.

```python
import math
import jax
import jax.numpy as jnp
import numpy as np
from jax import lax

MODEL_WIDTH = 1024
HEADS = 16
HEAD = 64
FF = 4096
LAYERS = 2
SEQUENCES = 4
LENGTH = 512


def shard_levels(own_key, extent, cuts, smallest, largest):
    def one(position, parts):
        heights = jax.random.uniform(jax.random.fold_in(jax.random.fold_in(own_key, 6), position), (parts,), jnp.float32, smallest / len(cuts), largest / len(cuts))
        return jnp.repeat(jnp.exp(heights), extent[position] // parts).reshape((-1,) + (1,) * (len(extent) - position - 1))

    loudness = one(*cuts[0])
    for cut in cuts[1:]:
        loudness = loudness * one(*cut)
    return loudness


def length_profile(number_of, total, most, skew):
    loads = [(1 << 20) // math.isqrt(grade ** skew) + 1 for grade in range(2, number_of + 1)]
    rest, given = total - most - (number_of - 1), [1] * (number_of - 1)
    while rest > 0:
        free = [i for i in range(number_of - 1) if given[i] < most]
        pool, left = sum([loads[i] for i in free]), rest
        for i in free:
            extra = min(most - given[i], max(1, left * loads[i] // pool), rest)
            given[i] = given[i] + extra
            rest = rest - extra
    return np.array([most] + given)


def ragged(rng, count, total, reach, skew):
    if count == 2:
        one = jax.random.randint(rng, (), max(1, total - reach), min(reach, total - 1) + 1)
        return jnp.stack([one, total - one])
    tallies = jnp.asarray(length_profile(count, total, reach, skew), jnp.int32)
    couples = (count - 1) // 2
    source_of, sink = tallies[1:1 + 2 * couples:2], tallies[2:2 + 2 * couples:2]
    margin = jnp.minimum(source_of - 1, reach - sink)
    moved = jax.random.randint(jax.random.fold_in(rng, 1), (couples,), 0, 1 << 20) % (margin + 1)
    tallies = tallies.at[1:1 + 2 * couples:2].set(source_of - moved).at[2:2 + 2 * couples:2].set(sink + moved)
    return tallies[jax.random.permutation(jax.random.fold_in(rng, 2), count)]


def scatter_about(key, shape, scale, bound, cuts=(), held_as=jnp.bfloat16):
    factor_of = shard_levels(key, shape, cuts, -0.22, 0.18) if cuts else 1.0
    result = jax.random.normal(key, shape, jnp.float32) * scale * factor_of
    return jnp.minimum(jnp.maximum(result, -bound), bound).astype(held_as)


def setup_inputs(seed: int = 0) -> dict:
    streams_of = jax.random.split(jax.random.key(seed), 10)
    hidden_in = scatter_about(streams_of[0], (SEQUENCES, LENGTH, MODEL_WIDTH), 1.0, 6.0, ((0, 2), (1, 4)))
    segment_ids = jax.vmap(lambda own: jnp.searchsorted(jnp.cumsum(ragged(own, max(3, LENGTH // 128), LENGTH, LENGTH // 2, 2)), jnp.arange(LENGTH), side="right"))(jax.random.split(streams_of[1], SEQUENCES)).reshape((SEQUENCES, LENGTH)).astype(jnp.int32)
    gains = jnp.clip(1.0 + 0.1 * jax.random.normal(streams_of[2], (LAYERS, 2, MODEL_WIDTH), jnp.float32), 0.5, 1.5).astype(jnp.bfloat16)
    biases = scatter_about(streams_of[3], (LAYERS, 10, MODEL_WIDTH), 0.5, 3.0, ((2, 32),))
    w_qkv = scatter_about(streams_of[4], (LAYERS, MODEL_WIDTH, 3, MODEL_WIDTH), MODEL_WIDTH ** -0.5, 0.1875, ((1, 8), (3, 4)))
    w_out_t = scatter_about(streams_of[5], (LAYERS, MODEL_WIDTH, MODEL_WIDTH), (MODEL_WIDTH // 8) ** -0.5, 0.5, ((1, 8), (2, 4)))
    w_up = scatter_about(streams_of[6], (LAYERS, MODEL_WIDTH, FF), MODEL_WIDTH ** -0.5, 0.1875, ((1, 8), (2, 4)))
    w_down_t = scatter_about(streams_of[7], (LAYERS, MODEL_WIDTH, FF), FF ** -0.5, 0.09375, ((1, 8), (2, 4)))
    grad_out = scatter_about(streams_of[8], (SEQUENCES, LENGTH, MODEL_WIDTH), 1.0, 6.0, ((0, 2), (1, 4)))
    return dict(hidden_in=hidden_in, segment_ids=segment_ids, gains=gains, biases=biases, w_qkv=w_qkv, w_out_t=w_out_t, w_up=w_up, w_down_t=w_down_t, grad_out=grad_out)


EPS = 1e-05
GELU_C = 0.7978845608028654
GELU_K = 0.044715

def rounded(values):
    return lax.optimization_barrier(values.astype(jnp.bfloat16)).astype(jnp.float32)

def norm_parts(values):
    center = values - lax.optimization_barrier(jnp.mean(values, -1, keepdims=True))
    inverse = lax.rsqrt(lax.optimization_barrier(jnp.mean(center * center, -1, keepdims=True)) + EPS)
    return (center * inverse, inverse)

def norm_back(grad_y, normed, inverse, gain):
    scaled = grad_y * gain
    return inverse * (scaled - lax.optimization_barrier(jnp.mean(scaled, -1, keepdims=True)) - normed * lax.optimization_barrier(jnp.mean(scaled * normed, -1, keepdims=True)))

def gelu_parts(values):
    bend = jnp.tanh(GELU_C * (values + GELU_K * values * values * values))
    return (0.5 * values * (1.0 + bend), bend)

def gelu_slope(values, bend):
    return 0.5 * (1.0 + bend) + 0.5 * values * (1.0 - bend * bend) * GELU_C * (1.0 + 3.0 * GELU_K * values * values)

def attention_rows(query, keys, seg, start, slope):
    rows = query.shape[0]
    length = keys.shape[0]
    q_pos = start + jnp.arange(rows, dtype=jnp.int32)
    k_pos = jnp.arange(length, dtype=jnp.int32)
    q_seg = lax.dynamic_slice_in_dim(seg, start, rows, 0)
    mask = (k_pos[None, :] <= q_pos[:, None]) & (seg[None, :] == q_seg[:, None])
    dist = (q_pos[:, None] - k_pos[None, :]).astype(jnp.float32)
    scale = 1.0 / math.sqrt(HEAD)
    score = jnp.einsum('qhd,khd->hqk', query.astype(jnp.float32), keys.astype(jnp.float32)) * scale - slope[:, None, None] * dist[None]
    return (score, mask[None])

def attention_forward(query_key_value, seg, slope):
    length = query_key_value.shape[0]
    rows = min(512, length)

    def one(index):
        start = index * rows
        query = lax.dynamic_slice_in_dim(query_key_value[:, 0], start, rows, 0)
        score, mask = attention_rows(query, query_key_value[:, 1], seg, start, slope)
        expo = jnp.where(mask, jnp.exp(jnp.where(mask, score, 0.0)), 0.0)
        total = lax.optimization_barrier(jnp.sum(expo, -1))
        summed = jnp.einsum('hqk,khd->qhd', rounded(expo), query_key_value[:, 2].astype(jnp.float32))
        out = summed / jnp.transpose(total)[:, :, None]
        return (out.astype(jnp.bfloat16), jnp.log(total))
    outs, lses = lax.map(one, jnp.arange(length // rows, dtype=jnp.int32))
    return (outs.reshape(length, HEADS, HEAD), jnp.transpose(lses, (1, 0, 2)).reshape(HEADS, length))

def attention_backward(query_key_value, seg, ctx, lse, dctx, slope):
    length = query_key_value.shape[0]
    rows = min(512, length)
    scale = 1.0 / math.sqrt(HEAD)
    keys = query_key_value[:, 1].astype(jnp.float32)
    values = query_key_value[:, 2].astype(jnp.float32)

    def step(carry, index):
        dkey, dvalue = carry
        start = index * rows
        query = lax.dynamic_slice_in_dim(query_key_value[:, 0], start, rows, 0)
        score, mask = attention_rows(query, query_key_value[:, 1], seg, start, slope)
        lse_rows = lax.dynamic_slice_in_dim(lse, start, rows, 1)
        prob = jnp.where(mask, jnp.exp(jnp.where(mask, score - lse_rows[:, :, None], 0.0)), 0.0)
        dctx_rows = lax.dynamic_slice_in_dim(dctx, start, rows, 0).astype(jnp.float32)
        ctx_rows = lax.dynamic_slice_in_dim(ctx, start, rows, 0).astype(jnp.float32)
        dvalue = dvalue + jnp.einsum('hqk,qhd->khd', rounded(prob), dctx_rows)
        dprob = jnp.einsum('qhd,khd->hqk', dctx_rows, values)
        delta = jnp.transpose(lax.optimization_barrier(jnp.sum(dctx_rows * ctx_rows, -1)))
        dscore = rounded(prob * (dprob - delta[:, :, None]))
        dquery = jnp.einsum('hqk,khd->qhd', dscore, keys) * scale
        dkey = dkey + jnp.einsum('hqk,qhd->khd', dscore, query.astype(jnp.float32)) * scale
        return ((dkey, dvalue), dquery)
    zeros = jnp.zeros((length, HEADS, HEAD), jnp.float32)
    (dkey, dvalue), dquery = lax.scan(step, (zeros, zeros), jnp.arange(length // rows, dtype=jnp.int32))
    return (dquery.reshape(length, HEADS, HEAD), dkey, dvalue)

def layer_forward(x, gain, bias, wqkv, wout, wup, wdown, seg, slope):
    normed1, inverse1 = norm_parts(x)
    first_activation = (normed1 * gain[0] + bias[0]).astype(jnp.bfloat16)
    query_key_value = jnp.dot(first_activation.reshape(-1, MODEL_WIDTH), wqkv.reshape(MODEL_WIDTH, 3 * MODEL_WIDTH), preferred_element_type=jnp.float32).reshape(-1, 3, MODEL_WIDTH)
    shift = jnp.stack([bias[2], jnp.zeros_like(bias[2]), bias[3]])
    heads = (query_key_value + shift).astype(jnp.bfloat16).reshape(SEQUENCES, LENGTH, 3, HEADS, HEAD)
    ctx, lse = lax.map(lambda pair: attention_forward(pair[0], pair[1], slope), (heads, seg))
    attn = jnp.dot(ctx.reshape(-1, MODEL_WIDTH), wout.T, preferred_element_type=jnp.float32).reshape(x.shape)
    x2 = x + attn + bias[4]
    normed2, inverse2 = norm_parts(x2)
    second_activation = (normed2 * gain[1] + bias[1]).astype(jnp.bfloat16)
    up_projected = jnp.dot(second_activation.reshape(-1, MODEL_WIDTH), wup, preferred_element_type=jnp.float32) + bias[6:].reshape(FF)
    act, bend = gelu_parts(up_projected)
    act_bf = act.astype(jnp.bfloat16)
    down = jnp.dot(act_bf, wdown.T, preferred_element_type=jnp.float32).reshape(x.shape)
    return (x2 + down + bias[5], (x, first_activation, heads, ctx, lse, x2, second_activation, up_projected, act_bf))

def layer_backward(saved, grad_y, gain, bias, wqkv, wout, wup, wdown, seg, slope):
    x, first_activation, heads, ctx, lse, x2, second_activation, up_projected, act_bf = saved
    grad_flat = grad_y.reshape(-1, MODEL_WIDTH)
    grad_bf = grad_flat.astype(jnp.bfloat16)
    grad_bd = lax.optimization_barrier(jnp.sum(grad_flat, 0))
    grad_wd = jnp.dot(grad_bf.T, act_bf, preferred_element_type=jnp.float32)
    dact = jnp.dot(grad_bf, wdown, preferred_element_type=jnp.float32)
    _, bend = gelu_parts(up_projected)
    dup = dact * gelu_slope(up_projected, bend)
    grad_bu = lax.optimization_barrier(jnp.sum(dup, 0))
    up_gradient_half_precision = dup.astype(jnp.bfloat16)
    up_weight_gradient = jnp.dot(second_activation.reshape(-1, MODEL_WIDTH).T, up_gradient_half_precision, preferred_element_type=jnp.float32)
    da2 = jnp.dot(up_gradient_half_precision, wup.T, preferred_element_type=jnp.float32)
    normed2, inverse2 = norm_parts(x2.reshape(-1, MODEL_WIDTH))
    grad_g2 = lax.optimization_barrier(jnp.sum(da2 * normed2, 0))
    grad_b2 = lax.optimization_barrier(jnp.sum(da2, 0))
    gx2 = grad_flat + norm_back(da2, normed2, inverse2, gain[1])
    grad_bo = lax.optimization_barrier(jnp.sum(gx2, 0))
    gx2_bf = gx2.astype(jnp.bfloat16)
    grad_wo = jnp.dot(gx2_bf.T, ctx.reshape(-1, MODEL_WIDTH), preferred_element_type=jnp.float32)
    dctx = jnp.dot(gx2_bf, wout, preferred_element_type=jnp.float32).astype(jnp.bfloat16).reshape(SEQUENCES, LENGTH, HEADS, HEAD)
    dq, dk, value_gradient = lax.map(lambda item: attention_backward(item[0], item[1], item[2], item[3], item[4], slope), (heads, seg, ctx, lse, dctx))
    query_gradient_flat = dq.reshape(-1, MODEL_WIDTH)
    key_gradient_flat = dk.reshape(-1, MODEL_WIDTH)
    value_gradient_flat = value_gradient.reshape(-1, MODEL_WIDTH)
    grad_bq = lax.optimization_barrier(jnp.sum(query_gradient_flat, 0))
    value_bias_gradient = lax.optimization_barrier(jnp.sum(value_gradient_flat, 0))
    packed_projection_gradient = jnp.stack([query_gradient_flat, key_gradient_flat, value_gradient_flat], 1).astype(jnp.bfloat16).reshape(-1, 3 * MODEL_WIDTH)
    grad_wqkv = jnp.dot(first_activation.reshape(-1, MODEL_WIDTH).T, packed_projection_gradient, preferred_element_type=jnp.float32).reshape(MODEL_WIDTH, 3, MODEL_WIDTH)
    da1 = jnp.dot(packed_projection_gradient, wqkv.reshape(MODEL_WIDTH, 3 * MODEL_WIDTH).T, preferred_element_type=jnp.float32)
    normed1, inverse1 = norm_parts(x.reshape(-1, MODEL_WIDTH))
    grad_g1 = lax.optimization_barrier(jnp.sum(da1 * normed1, 0))
    grad_b1 = lax.optimization_barrier(jnp.sum(da1, 0))
    grad_x = gx2 + norm_back(da1, normed1, inverse1, gain[0])
    grad_gain = jnp.stack([grad_g1, grad_g2])
    grad_bias = jnp.concatenate([jnp.stack([grad_b1, grad_b2, grad_bq, value_bias_gradient, grad_bo, grad_bd]), grad_bu.reshape(FF // MODEL_WIDTH, MODEL_WIDTH)], 0)
    return (grad_x.reshape(grad_y.shape), grad_gain, grad_bias, grad_wqkv, grad_wo, up_weight_gradient, grad_wd)

def reference(hidden_in, segment_ids, gains, biases, w_qkv, w_out_t, w_up, w_down_t, grad_out):
    slope = jnp.exp2(-8.0 * (jnp.arange(HEADS, dtype=jnp.int32).astype(jnp.float32) + 1.0) / HEADS)
    state = hidden_in.astype(jnp.float32)
    saves = []
    for layer in range(LAYERS):
        state, saved = layer_forward(state, gains[layer], biases[layer], w_qkv[layer], w_out_t[layer], w_up[layer], w_down_t[layer], segment_ids, slope)
        saves.append(saved)
    output = state.astype(jnp.bfloat16)
    grad = grad_out.astype(jnp.float32)
    results = []
    for layer in reversed(range(LAYERS)):
        outcome = layer_backward(saves[layer], grad, gains[layer], biases[layer], w_qkv[layer], w_out_t[layer], w_up[layer], w_down_t[layer], segment_ids, slope)
        grad = outcome[0]
        results.insert(0, outcome[1:])
    grad_gains = jnp.stack([item[0] for item in results])
    grad_biases = jnp.stack([item[1] for item in results])
    grad_qkv = jnp.stack([item[2] for item in results])
    grad_attn_out = jnp.stack([item[3] for item in results])
    grad_up = jnp.stack([item[4] for item in results])
    grad_down = jnp.stack([item[5] for item in results])
    return (output, grad.astype(jnp.bfloat16), grad_gains, grad_biases, grad_qkv, grad_attn_out, grad_up, grad_down)
```

```python
import math

import jax
import jax.numpy as jnp
from jax import lax
from jax.experimental import pallas as pl
from jax.experimental.pallas import tpu as pltpu
from jax.sharding import PartitionSpec as P

HEADS = 16
HEAD = 64


EPS = 1e-05
GELU_C = 0.7978845608028654
GELU_K = 0.044715


def norm_parts(values):
    center = values - jnp.mean(values, -1, keepdims=True)
    inverse = lax.rsqrt(jnp.mean(center * center, -1, keepdims=True) + EPS)
    return (center * inverse, inverse)


def norm_back(grad_y, normed, inverse, gain):
    scaled = grad_y * gain
    return inverse * (
        scaled
        - jnp.mean(scaled, -1, keepdims=True)
        - normed * jnp.mean(scaled * normed, -1, keepdims=True)
    )


def gelu_parts(values):
    bend = jnp.tanh(GELU_C * (values + GELU_K * values * values * values))
    return (0.5 * values * (1.0 + bend), bend)


def gelu_slope(values, bend):
    return 0.5 * (1.0 + bend) + 0.5 * values * (1.0 - bend * bend) * GELU_C * (
        1.0 + 3.0 * GELU_K * values * values
    )


MESH = pl.DeviceIdType.MESH
ANY = pl.BlockSpec(memory_space=pl.ANY)
VMEM = pl.BlockSpec(memory_space=pltpu.VMEM)


def rank_of(kind):
    if kind in ("mp", "ctx"):
        return lax.axis_index(kind), lax.axis_size(kind)
    count = lax.axis_size("ctx")
    if kind == "core":
        return lax.rem(lax.axis_index("ctx"), 2), 2
    flat = lax.axis_index("batch") * count + lax.axis_index("ctx")
    if kind == "chip":
        return flat // 2, lax.axis_size("batch") * count // 2
    return flat, lax.axis_size("batch") * count


def device_of(kind, rank):
    if kind in ("mp", "ctx"):
        return {kind: rank}
    count = lax.axis_size("ctx")
    if kind == "core":
        return {"ctx": (lax.axis_index("ctx") // 2) * 2 + rank}
    flat = rank * 2 + lax.rem(lax.axis_index("ctx"), 2)
    return {"batch": flat // count, "ctx": lax.rem(flat, count)}


def greet(devices):
    barrier = pltpu.get_barrier_semaphore()
    for device in devices:
        pl.semaphore_signal(barrier, inc=1, device_id=device, device_id_type=MESH)
    pl.semaphore_wait(barrier, len(devices))


def remote(src, dst, send, recv, device):
    return pltpu.make_async_remote_copy(
        src_ref=src, dst_ref=dst, send_sem=send, recv_sem=recv,
        device_id=device, device_id_type=MESH,
    )


def total_mp(values, name):
    rows, width = values.shape
    count = lax.axis_size("mp")
    piece = rows // count

    def kernel(x_ref, o_ref, held, send, recv):
        me, _ = rank_of("mp")
        ranks = [lax.rem(me + t, count) for t in range(1, count)]
        devices = [device_of("mp", rank) for rank in ranks]
        greet(devices)
        mine = pl.ds(pl.multiple_of(me * piece, piece), piece)
        first = []
        for t in range(count - 1):
            theirs = pl.ds(pl.multiple_of(ranks[t] * piece, piece), piece)
            copy = remote(x_ref.at[theirs], held.at[t], send.at[0, t], recv.at[0, t], devices[t])
            copy.start()
            first.append(copy)
        acc = x_ref[mine, :].astype(jnp.float32)
        for t in range(count - 1):
            first[t].wait_recv()
            acc = acc + held[t].astype(jnp.float32)
        o_ref[mine, :] = acc.astype(jnp.bfloat16)
        second = []
        for t in range(count - 1):
            copy = remote(o_ref.at[mine], o_ref.at[mine], send.at[1, t], recv.at[1, t], devices[t])
            copy.start()
            second.append(copy)
        for copy in first:
            copy.wait_send()
        for copy in second:
            copy.wait_send()
        for t in range(count - 1):
            source = lax.rem(me + count - 1 - t, count)
            theirs = pl.ds(pl.multiple_of(source * piece, piece), piece)
            remote(
                o_ref.at[theirs], o_ref.at[theirs], send.at[1, t], recv.at[1, t], devices[t]
            ).wait_recv()

    return pl.pallas_call(
        kernel,
        out_shape=jax.ShapeDtypeStruct((rows, width), jnp.bfloat16),
        in_specs=[VMEM],
        out_specs=VMEM,
        scratch_shapes=[
            pltpu.VMEM((count - 1, piece, width), jnp.bfloat16),
            pltpu.SemaphoreType.DMA((2, count - 1)),
            pltpu.SemaphoreType.DMA((2, count - 1)),
        ],
        compiler_params=pltpu.CompilerParams(collective_id=0, has_side_effects=True),
        name="total_mp",
    )(values)


def spread(arrays, kind, ident):
    me, count = rank_of(kind)
    size = len(arrays)

    def kernel(*refs):
        ins, outs, (send, recv) = refs[:size], refs[size : 2 * size], refs[2 * size :]
        rank, _ = rank_of(kind)
        devices = [device_of(kind, lax.rem(rank + t, count)) for t in range(1, count)]
        greet(devices)
        copies = []
        for t in range(count - 1):
            for i in range(size):
                copy = remote(ins[i], outs[i].at[rank], send.at[i, t], recv.at[i, t], devices[t])
                copy.start()
                copies.append(copy)
        for copy in copies:
            copy.wait_send()
        for t in range(count - 1):
            source = lax.rem(rank + count - 1 - t, count)
            for i in range(size):
                remote(
                    ins[i], outs[i].at[source], send.at[i, t], recv.at[i, t], devices[t]
                ).wait_recv()

    outs = pl.pallas_call(
        kernel,
        out_shape=[jax.ShapeDtypeStruct((count,) + a.shape, a.dtype) for a in arrays],
        in_specs=[ANY] * size,
        out_specs=[ANY] * size,
        scratch_shapes=[pltpu.SemaphoreType.DMA((size, count - 1))] * 2,
        compiler_params=pltpu.CompilerParams(collective_id=ident, has_side_effects=True),
        name="spread_" + kind,
    )(*arrays)
    return [lax.dynamic_update_index_in_dim(o, a, me, 0) for o, a in zip(outs, arrays)]


def spread_all(arrays, ident):
    me, total = rank_of("flat")
    size = len(arrays)
    chips = total // 2

    def kernel(*refs):
        ins, outs, (send, recv, send2, recv2) = refs[:size], refs[size : 2 * size], refs[2 * size :]
        chip, _ = rank_of("chip")
        core, _ = rank_of("core")
        rank = chip * 2 + core
        other = chip * 2 + 1 - core
        devices = [device_of("chip", lax.rem(chip + t, chips)) for t in range(1, chips)]
        sibling = device_of("core", 1 - core)
        greet(devices + [sibling])
        sent = []
        for i in range(size):
            for t in range(chips - 1):
                copy = remote(ins[i], outs[i].at[rank], send.at[i, t], recv.at[i, t], devices[t])
                copy.start()
                sent.append(copy)
        for i in range(size):
            copy = remote(
                ins[i], outs[i].at[rank], send2.at[i, 0], recv2.at[i, 0], sibling
            )
            copy.start()
            sent.append(copy)
        for i in range(size):
            for t in range(chips - 1):
                source = lax.rem(chip + chips - 1 - t, chips) * 2 + core
                remote(
                    ins[i], outs[i].at[source], send.at[i, t], recv.at[i, t], devices[t]
                ).wait_recv()
                copy = remote(
                    outs[i].at[source], outs[i].at[source],
                    send2.at[i, t + 1], recv2.at[i, t + 1], sibling,
                )
                copy.start()
                sent.append(copy)
        for copy in sent:
            copy.wait_send()
        for i in range(size):
            remote(
                ins[i], outs[i].at[other], send2.at[i, 0], recv2.at[i, 0], sibling
            ).wait_recv()
            for t in range(chips - 1):
                source = lax.rem(chip + chips - 1 - t, chips) * 2 + 1 - core
                remote(
                    ins[i], outs[i].at[source],
                    send2.at[i, t + 1], recv2.at[i, t + 1], sibling,
                ).wait_recv()

    outs = pl.pallas_call(
        kernel,
        out_shape=[jax.ShapeDtypeStruct((total,) + a.shape, a.dtype) for a in arrays],
        in_specs=[ANY] * size,
        out_specs=[ANY] * size,
        scratch_shapes=[pltpu.SemaphoreType.DMA((size, chips - 1))] * 2
        + [pltpu.SemaphoreType.DMA((size, chips))] * 2,
        compiler_params=pltpu.CompilerParams(collective_id=ident, has_side_effects=True),
        name="spread_all",
    )(*arrays)
    return [lax.dynamic_update_index_in_dim(o, a, me, 0) for o, a in zip(outs, arrays)]


def trade(arrays, kind, ident, dim=0):
    me, count = rank_of(kind)
    size = len(arrays)

    def pick(ref, rank):
        return ref.at[rank] if dim == 0 else ref.at[:, rank]

    def kernel(*refs):
        ins, outs, (send, recv) = refs[:size], refs[size : 2 * size], refs[2 * size :]
        rank, _ = rank_of(kind)
        ranks = [lax.rem(rank + t, count) for t in range(1, count)]
        devices = [device_of(kind, peer) for peer in ranks]
        greet(devices)
        copies = []
        for t in range(count - 1):
            for i in range(size):
                copy = remote(
                    pick(ins[i], ranks[t]), outs[i].at[t], send.at[i, t], recv.at[i, t], devices[t]
                )
                copy.start()
                copies.append(copy)
        for copy in copies:
            copy.wait()

    def shape_of(a):
        return (count - 1,) + a.shape[:dim] + a.shape[dim + 1 :]

    outs = pl.pallas_call(
        kernel,
        out_shape=[jax.ShapeDtypeStruct(shape_of(a), a.dtype) for a in arrays],
        in_specs=[ANY] * size,
        out_specs=[ANY] * size,
        scratch_shapes=[pltpu.SemaphoreType.DMA((size, count - 1))] * 2,
        compiler_params=pltpu.CompilerParams(collective_id=ident, has_side_effects=True),
        name="trade_" + kind,
    )(*arrays)
    sums = []
    for got, a in zip(outs, arrays):
        acc = lax.dynamic_index_in_dim(a, me, dim, keepdims=False).astype(jnp.float32)
        for t in range(count - 1):
            acc = acc + got[t].astype(jnp.float32)
        sums.append(acc)
    return sums


def scatter_all(arrays, ident):
    _, total = rank_of("flat")
    split = [a.reshape((total // 2, 2, a.shape[0] // total) + a.shape[1:]) for a in arrays]
    halves = trade(split, "core", ident, dim=1)
    return trade([h.astype(a.dtype) for h, a in zip(halves, arrays)], "chip", ident + 1)


def block_mask(q_pos, q_seg, key_seg, start, block):
    k_pos = start + jnp.arange(block, dtype=jnp.int32)
    seg_keys = lax.dynamic_slice_in_dim(key_seg, start, block, 1)
    mask = (k_pos[None, None, :] <= q_pos[None, :, None]) & (
        seg_keys[:, None, :] == q_seg[:, :, None]
    )
    return mask[:, None]


def block_scores(query, keys, q_pos, start, block, slope, scale):
    k_pos = start + jnp.arange(block, dtype=jnp.int32)
    dist = (q_pos[:, None] - k_pos[None, :]).astype(jnp.float32)
    score = jnp.einsum("sqhd,skhd->shqk", query, keys, preferred_element_type=jnp.float32)
    return score * scale - slope[None, :, None, None] * dist[None, None]


def attend_forward(query, kv_all, q_pos, q_seg, key_seg, slope):
    seqs, rows, heads, width = query.shape
    length = kv_all.shape[1]
    block = min(512, length)
    scale = 1.0 / math.sqrt(width)

    def step(carry, index):
        start = index * block
        mask = block_mask(q_pos, q_seg, key_seg, start, block)

        def work(state):
            acc, total = state
            pair = lax.dynamic_slice_in_dim(kv_all, start, block, 1).reshape(
                seqs, block, 2, heads, width
            )
            score = block_scores(query, pair[:, :, 0], q_pos, start, block, slope, scale)
            expo = jnp.where(mask, jnp.exp(jnp.where(mask, score, 0.0)), 0.0)
            acc = acc + jnp.einsum(
                "shqk,skhd->sqhd",
                expo.astype(jnp.bfloat16),
                pair[:, :, 1],
                preferred_element_type=jnp.float32,
            )
            return (acc, total + jnp.sum(expo, -1))

        if length == block:
            return (work(carry), None)
        return (lax.cond(jnp.any(mask), work, lambda state: state, carry), None)

    init = (jnp.zeros(query.shape, jnp.float32), jnp.zeros((seqs, heads, rows), jnp.float32))
    if length == block:
        (acc, total), _ = step(init, 0)
    else:
        (acc, total), _ = lax.scan(step, init, jnp.arange(length // block, dtype=jnp.int32))
    ctx = (acc / jnp.transpose(total, (0, 2, 1))[..., None]).astype(jnp.bfloat16)
    return (ctx, jnp.log(total))


def attend_backward(query, kv_all, q_pos, q_seg, key_seg, slope, ctx, lse, dctx):
    seqs, rows, heads, width = query.shape
    length = kv_all.shape[1]
    block = min(512, length)
    scale = 1.0 / math.sqrt(width)
    delta = jnp.transpose(
        jnp.sum(dctx.astype(jnp.float32) * ctx.astype(jnp.float32), -1), (0, 2, 1)
    )

    def step(carry, index):
        start = index * block
        mask = block_mask(q_pos, q_seg, key_seg, start, block)

        def work(state):
            grad_q, grad_kv = state
            pair = lax.dynamic_slice_in_dim(kv_all, start, block, 1).reshape(
                seqs, block, 2, heads, width
            )
            score = block_scores(query, pair[:, :, 0], q_pos, start, block, slope, scale)
            prob = jnp.where(mask, jnp.exp(jnp.where(mask, score - lse[..., None], 0.0)), 0.0)
            grad_v = jnp.einsum(
                "shqk,sqhd->skhd",
                prob.astype(jnp.bfloat16),
                dctx,
                preferred_element_type=jnp.float32,
            )
            grad_p = jnp.einsum(
                "sqhd,skhd->shqk", dctx, pair[:, :, 1], preferred_element_type=jnp.float32
            )
            grad_s = (prob * (grad_p - delta[..., None])).astype(jnp.bfloat16)
            grad_q = (
                grad_q
                + jnp.einsum(
                    "shqk,skhd->sqhd", grad_s, pair[:, :, 0], preferred_element_type=jnp.float32
                )
                * scale
            )
            grad_k = (
                jnp.einsum("shqk,sqhd->skhd", grad_s, query, preferred_element_type=jnp.float32)
                * scale
            )
            piece = jnp.stack([grad_k, grad_v], 2).reshape(seqs, block, 2, heads * width)
            if length == block:
                return (grad_q, piece)
            return (grad_q, lax.dynamic_update_slice_in_dim(grad_kv, piece, start, 1))

        if length == block:
            return (work(carry), None)
        return (lax.cond(jnp.any(mask), work, lambda state: state, carry), None)

    init = (
        jnp.zeros(query.shape, jnp.float32),
        jnp.zeros((seqs, length, 2, heads * width), jnp.float32),
    )
    if length == block:
        (grad_q, grad_kv), _ = step(init, 0)
    else:
        (grad_q, grad_kv), _ = lax.scan(step, init, jnp.arange(length // block, dtype=jnp.int32))
    return (grad_q, grad_kv)


def per_device(hidden_in, segment_ids, gains, biases, w_qkv, w_out_t, w_up, w_down_t, grad_out):
    seqs, rows, width = hidden_in.shape
    layers = w_qkv.shape[0]
    cols = w_qkv.shape[3]
    ff_cols = w_up.shape[2]
    heads = cols // HEAD
    mp_count = lax.axis_size("mp")
    mp_index = lax.axis_index("mp")
    layers_rows = gains.shape[0] * gains.shape[1]
    bias_count = biases.shape[0] * biases.shape[1]
    part = gains.shape[2]
    vectors = jnp.concatenate(
        [gains.reshape(layers_rows, part), biases.reshape(bias_count, part)], 0
    )
    (vectors,) = spread([vectors], "mp", 1)
    first = spread_all(
        [
            w_qkv[0].reshape(-1, 3 * cols),
            w_out_t[0],
            w_up[0],
            w_down_t[0],
            vectors.reshape(-1, part),
            segment_ids,
        ],
        2,
    )
    owners = first[4].shape[0]
    vectors = jnp.transpose(
        first[4].reshape(owners, mp_count, layers_rows + bias_count, part), (2, 0, 1, 3)
    ).reshape(layers_rows + bias_count, width)
    all_gains = vectors[:layers_rows].reshape(gains.shape[:2] + (width,))
    all_biases = vectors[layers_rows:].reshape(biases.shape[:2] + (width,))
    ctx_count = lax.axis_size("ctx")
    key_seg = lax.dynamic_slice_in_dim(
        first[5], lax.axis_index("batch") * ctx_count, ctx_count, 0
    )
    key_seg = jnp.transpose(key_seg, (1, 0, 2)).reshape(seqs, ctx_count * rows)
    first_weights = (
        first[0].reshape(width, 3, cols),
        first[1].reshape(width, cols),
        first[2].reshape(width, ff_cols),
        first[3].reshape(width, ff_cols),
    )

    def sum_mp(values):
        flat = values.reshape(seqs * rows, width).astype(jnp.bfloat16)
        return total_mp(flat, "mp").reshape(values.shape).astype(jnp.float32)

    q_pos = lax.axis_index("ctx") * rows + jnp.arange(rows, dtype=jnp.int32)
    head_ids = (mp_index * heads + jnp.arange(heads, dtype=jnp.int32)).astype(jnp.float32)
    slope = jnp.exp2(-8.0 * (head_ids + 1.0) / HEADS)
    own = (jnp.arange(width, dtype=jnp.int32) // cols == mp_index).astype(jnp.float32)
    full_ff = ff_cols * mp_count

    def place(values, offset, total):
        return lax.dynamic_update_slice_in_dim(jnp.zeros((total,), jnp.float32), values, offset, 0)

    def unpack(layer):
        vec = all_biases[layer]
        query_bias = lax.dynamic_slice_in_dim(vec[2], mp_index * cols, cols, 0)
        value_bias = lax.dynamic_slice_in_dim(vec[3], mp_index * cols, cols, 0)
        up_projection_bias = lax.dynamic_slice_in_dim(
            vec[6:].reshape(-1), mp_index * ff_cols, ff_cols, 0
        )
        return (vec, query_bias, value_bias, up_projection_bias)

    def forward_layer(layer, state, weights):
        query_weight, w_o, up_weight, w_d = weights
        vec, query_bias, value_bias, up_projection_bias = unpack(layer)
        normed1, _ = norm_parts(state)
        first_activation = (normed1 * all_gains[layer, 0] + vec[0]).astype(jnp.bfloat16)
        query_key_value = jnp.einsum(
            "bph,hue->bpue", first_activation, query_weight, preferred_element_type=jnp.float32
        )
        shift = jnp.stack([query_bias, jnp.zeros_like(query_bias), value_bias])
        qkv_bf = (query_key_value + shift).astype(jnp.bfloat16)
        (kv_all,) = spread([qkv_bf[:, :, 1:].reshape(seqs, rows, 2 * cols)], "ctx", 3)
        kv_all = jnp.transpose(kv_all, (1, 0, 2, 3)).reshape(seqs, -1, 2, cols)
        query = qkv_bf[:, :, 0].reshape(seqs, rows, heads, HEAD)
        ctx, lse = attend_forward(query, kv_all, q_pos, segment_ids, key_seg, slope)
        ctx_flat = ctx.reshape(seqs, rows, cols)
        part = jnp.einsum("slc,oc->slo", ctx_flat, w_o, preferred_element_type=jnp.float32)
        mid = state + sum_mp(part) + vec[4]
        normed2, _ = norm_parts(mid)
        second_activation = (normed2 * all_gains[layer, 1] + vec[1]).astype(jnp.bfloat16)
        up_projected = (
            jnp.einsum(
                "nhz,zb->nhb", second_activation, up_weight, preferred_element_type=jnp.float32
            )
            + up_projection_bias
        )
        act, _ = gelu_parts(up_projected)
        act_bf = act.astype(jnp.bfloat16)
        down = jnp.einsum("slf,of->slo", act_bf, w_d, preferred_element_type=jnp.float32)
        result = mid + sum_mp(down) + vec[5]
        return (
            result,
            (
                state,
                first_activation,
                qkv_bf,
                kv_all,
                ctx_flat,
                lse,
                mid,
                second_activation,
                up_projected,
                act_bf,
            ),
        )

    state = hidden_in.astype(jnp.float32)
    saves = []
    for layer in range(layers):
        weights = first_weights if layer == 0 else (
            lax.all_gather(w_qkv[layer], ("batch", "ctx"), axis=0, tiled=True),
            lax.all_gather(w_out_t[layer], ("batch", "ctx"), axis=0, tiled=True),
            lax.all_gather(w_up[layer], ("batch", "ctx"), axis=0, tiled=True),
            lax.all_gather(w_down_t[layer], ("batch", "ctx"), axis=0, tiled=True),
        )
        state, saved = forward_layer(layer, state, weights)
        saves.append((weights, saved))
    output = state.astype(jnp.bfloat16)
    grad = grad_out.astype(jnp.float32)
    gain_rows = [None] * layers
    bias_rows = [None] * layers
    matrix_grads = [None] * layers
    for layer in reversed(range(layers)):
        kept_weights, saved = saves[layer]
        (
            x_in,
            first_activation,
            qkv_bf,
            kv_kept,
            ctx_flat,
            lse,
            mid,
            second_activation,
            up_projected,
            act_bf,
        ) = saved
        query_weight, w_o, up_weight, w_d = kept_weights
        kv_all = kv_kept
        gain1 = all_gains[layer, 0]
        gain2 = all_gains[layer, 1]
        grad_bf = grad.astype(jnp.bfloat16)
        grad_bd = jnp.sum(grad, (0, 1))
        grad_wd = jnp.einsum("slo,slf->of", grad_bf, act_bf, preferred_element_type=jnp.float32)
        dact = jnp.einsum("slo,of->slf", grad_bf, w_d, preferred_element_type=jnp.float32)
        _, bend = gelu_parts(up_projected)
        dup = dact * gelu_slope(up_projected, bend)
        grad_bu = jnp.sum(dup, (0, 1))
        up_gradient_half_precision = dup.astype(jnp.bfloat16)
        up_weight_gradient = jnp.einsum(
            "qwi,qwn->in",
            second_activation,
            up_gradient_half_precision,
            preferred_element_type=jnp.float32,
        )
        da2 = sum_mp(
            jnp.einsum(
                "cju,xu->cjx",
                up_gradient_half_precision,
                up_weight,
                preferred_element_type=jnp.float32,
            )
        )
        normed2, inverse2 = norm_parts(mid)
        grad_g2 = jnp.sum(da2 * normed2, (0, 1))
        grad_b2 = jnp.sum(da2, (0, 1))
        gx2 = grad + norm_back(da2, normed2, inverse2, gain2)
        grad_bo = jnp.sum(gx2, (0, 1))
        gx2_bf = gx2.astype(jnp.bfloat16)
        grad_wo = jnp.einsum("slo,slc->oc", gx2_bf, ctx_flat, preferred_element_type=jnp.float32)
        dctx = jnp.einsum("slo,oc->slc", gx2_bf, w_o, preferred_element_type=jnp.float32).astype(
            jnp.bfloat16
        )
        query = qkv_bf[:, :, 0].reshape(seqs, rows, heads, HEAD)
        ctx_heads = ctx_flat.reshape(seqs, rows, heads, HEAD)
        dctx_heads = dctx.reshape(seqs, rows, heads, HEAD)
        grad_q, grad_kv_terms = attend_backward(
            query, kv_all, q_pos, segment_ids, key_seg, slope, ctx_heads, lse, dctx_heads
        )
        kv_terms = jnp.transpose(
            grad_kv_terms.astype(jnp.bfloat16).reshape(seqs, ctx_count, rows, 2 * cols),
            (1, 0, 2, 3),
        )
        grad_kv = trade([kv_terms], "ctx", 4)[0].reshape(seqs, rows, 2, cols)
        grad_qf = grad_q.reshape(seqs, rows, cols)
        grad_bq = jnp.sum(grad_qf, (0, 1))
        value_bias_gradient = jnp.sum(grad_kv[:, :, 1], (0, 1))
        packed_projection_gradient = jnp.concatenate([grad_qf[:, :, None], grad_kv], 2).astype(
            jnp.bfloat16
        )
        query_weight_gradient = jnp.einsum(
            "ebz,ebpy->zpy",
            first_activation,
            packed_projection_gradient,
            preferred_element_type=jnp.float32,
        )
        da1 = sum_mp(
            jnp.einsum(
                "aewu,vwu->aev",
                packed_projection_gradient,
                query_weight,
                preferred_element_type=jnp.float32,
            )
        )
        normed1, inverse1 = norm_parts(x_in)
        grad_g1 = jnp.sum(da1 * normed1, (0, 1))
        grad_b1 = jnp.sum(da1, (0, 1))
        grad = gx2 + norm_back(da1, normed1, inverse1, gain1)
        gain_rows[layer] = jnp.stack([grad_g1 * own, grad_g2 * own])
        head_rows = jnp.stack(
            [
                grad_b1 * own,
                grad_b2 * own,
                place(grad_bq, mp_index * cols, width),
                place(value_bias_gradient, mp_index * cols, width),
                grad_bo * own,
                grad_bd * own,
            ]
        )
        unit_rows = place(grad_bu, mp_index * ff_cols, full_ff).reshape(full_ff // width, width)
        bias_rows[layer] = jnp.concatenate([head_rows, unit_rows], 0)
        rounded = [
            item.astype(jnp.bfloat16)
            for item in (
                query_weight_gradient.reshape(width, 3 * cols),
                grad_wo,
                up_weight_gradient,
                grad_wd,
            )
        ]
        if layer:
            matrix_grads[layer] = [
                lax.psum_scatter(
                    item, ("batch", "ctx"), scatter_dimension=0, tiled=True
                ).astype(jnp.float32)
                for item in rounded
            ]
    row_count = layers_rows + bias_count
    terms = jnp.concatenate(
        [
            jnp.stack(gain_rows).reshape(layers_rows, width),
            jnp.stack(bias_rows).reshape(bias_count, width),
        ],
        0,
    ).reshape(row_count, owners, mp_count, part)
    terms = jnp.transpose(terms, (2, 0, 1, 3)).reshape(mp_count, row_count, owners * part)
    (terms,) = trade([terms], "mp", 5)
    terms = jnp.transpose(terms.reshape(row_count, owners, part), (1, 0, 2))
    *matrix_grads[0], terms = scatter_all(rounded + [terms.reshape(owners * row_count, part)], 6)
    grad_gains = terms[:layers_rows].reshape(gains.shape)
    grad_biases = terms[layers_rows:].reshape(biases.shape)
    grad_qkv = jnp.stack([item[0] for item in matrix_grads]).reshape(w_qkv.shape)
    grad_attn_out = jnp.stack([item[1] for item in matrix_grads])
    grad_up = jnp.stack([item[2] for item in matrix_grads])
    grad_down = jnp.stack([item[3] for item in matrix_grads])
    return (
        output,
        grad.astype(jnp.bfloat16),
        grad_gains,
        grad_biases,
        grad_qkv,
        grad_attn_out,
        grad_up,
        grad_down,
    )


def solution(mesh):
    in_specs = (
        P("batch", "ctx", None),
        P("batch", "ctx"),
        P(None, None, ("batch", "ctx", "mp")),
        P(None, None, ("batch", "ctx", "mp")),
        P(None, ("batch", "ctx"), None, "mp"),
        P(None, ("batch", "ctx"), "mp"),
        P(None, ("batch", "ctx"), "mp"),
        P(None, ("batch", "ctx"), "mp"),
        P("batch", "ctx", None),
    )
    out_specs = (
        P("batch", "ctx", None),
        P("batch", "ctx", None),
        P(None, None, ("batch", "ctx", "mp")),
        P(None, None, ("batch", "ctx", "mp")),
        P(None, ("batch", "ctx"), None, "mp"),
        P(None, ("batch", "ctx"), "mp"),
        P(None, ("batch", "ctx"), "mp"),
        P(None, ("batch", "ctx"), "mp"),
    )
    return jax.shard_map(
        per_device, mesh=mesh, in_specs=in_specs, out_specs=out_specs, check_vma=False
    )
```

```python
import math

import jax
import jax.numpy as jnp
from jax import lax
from jax.experimental import pallas as pl
from jax.experimental.pallas import tpu as pltpu
from jax.sharding import PartitionSpec as P

HEADS = 16
HEAD = 64


EPS = 1e-05
GELU_C = 0.7978845608028654
GELU_K = 0.044715


def norm_parts(values):
    center = values - jnp.mean(values, -1, keepdims=True)
    inverse = lax.rsqrt(jnp.mean(center * center, -1, keepdims=True) + EPS)
    return (center * inverse, inverse)


def norm_back(grad_y, normed, inverse, gain):
    scaled = grad_y * gain
    return inverse * (
        scaled
        - jnp.mean(scaled, -1, keepdims=True)
        - normed * jnp.mean(scaled * normed, -1, keepdims=True)
    )


def gelu_parts(values):
    bend = jnp.tanh(GELU_C * (values + GELU_K * values * values * values))
    return (0.5 * values * (1.0 + bend), bend)


def gelu_slope(values, bend):
    return 0.5 * (1.0 + bend) + 0.5 * values * (1.0 - bend * bend) * GELU_C * (
        1.0 + 3.0 * GELU_K * values * values
    )


MESH = pl.DeviceIdType.MESH
ANY = pl.BlockSpec(memory_space=pl.ANY)
VMEM = pl.BlockSpec(memory_space=pltpu.VMEM)


def rank_of(kind):
    if kind in ("mp", "ctx"):
        return lax.axis_index(kind), lax.axis_size(kind)
    count = lax.axis_size("ctx")
    if kind == "core":
        return lax.rem(lax.axis_index("ctx"), 2), 2
    flat = lax.axis_index("batch") * count + lax.axis_index("ctx")
    if kind == "chip":
        return flat // 2, lax.axis_size("batch") * count // 2
    return flat, lax.axis_size("batch") * count


def device_of(kind, rank):
    if kind in ("mp", "ctx"):
        return {kind: rank}
    count = lax.axis_size("ctx")
    if kind == "core":
        return {"ctx": (lax.axis_index("ctx") // 2) * 2 + rank}
    flat = rank * 2 + lax.rem(lax.axis_index("ctx"), 2)
    return {"batch": flat // count, "ctx": lax.rem(flat, count)}


def greet(devices):
    barrier = pltpu.get_barrier_semaphore()
    for device in devices:
        pl.semaphore_signal(barrier, inc=1, device_id=device, device_id_type=MESH)
    pl.semaphore_wait(barrier, len(devices))


def remote(src, dst, send, recv, device):
    return pltpu.make_async_remote_copy(
        src_ref=src, dst_ref=dst, send_sem=send, recv_sem=recv,
        device_id=device, device_id_type=MESH,
    )


def pick(ref, rank, dim):
    return ref.at[rank] if dim == 0 else ref.at[:, rank]


def cut(shape, dim):
    return shape[:dim] + shape[dim + 1 :]


def gathered(got, own, kind, dim):
    acc = lax.dynamic_index_in_dim(own, rank_of(kind)[0], dim, keepdims=False)
    acc = acc.astype(jnp.float32)
    for t in range(got.shape[0]):
        acc = acc + got[t].astype(jnp.float32)
    return acc


def total_mp(values, riders=(), ident=0):
    rows, width = values.shape
    size = len(riders)
    extra = [rank_of(kind)[1] - 1 for _, kind, _ in riders]
    count = lax.axis_size("mp")
    piece = rows // count

    def kernel(x_ref, *refs):
        loads, o_ref, lands = refs[:size], refs[size], refs[size + 1 : 2 * size + 1]
        held, send, recv, *pairs = refs[2 * size + 1 :]
        me, _ = rank_of("mp")
        ranks = [lax.rem(me + t, count) for t in range(1, count)]
        devices = [device_of("mp", rank) for rank in ranks]
        targets = {}
        for kind in sorted({kind for _, kind, _ in riders}):
            own, many = rank_of(kind)
            peers = [lax.rem(own + t, many) for t in range(1, many)]
            targets[kind] = [(peer, device_of(kind, peer)) for peer in peers]
        greet(devices + [d for group in targets.values() for _, d in group])
        mine = pl.ds(pl.multiple_of(me * piece, piece), piece)
        first = []
        for t in range(count - 1):
            theirs = pl.ds(pl.multiple_of(ranks[t] * piece, piece), piece)
            copy = remote(x_ref.at[theirs], held.at[t], send.at[0, t], recv.at[0, t], devices[t])
            copy.start()
            first.append(copy)
        carried = []
        for i, (_, kind, dim) in enumerate(riders):
            for t, (peer, device) in enumerate(targets[kind]):
                copy = remote(
                    pick(loads[i], peer, dim), lands[i].at[t],
                    pairs[2 * i].at[t], pairs[2 * i + 1].at[t], device,
                )
                copy.start()
                carried.append(copy)
        acc = x_ref[mine, :].astype(jnp.float32)
        for t in range(count - 1):
            first[t].wait_recv()
            acc = acc + held[t].astype(jnp.float32)
        o_ref[mine, :] = acc.astype(jnp.bfloat16)
        second = []
        for t in range(count - 1):
            copy = remote(o_ref.at[mine], o_ref.at[mine], send.at[1, t], recv.at[1, t], devices[t])
            copy.start()
            second.append(copy)
        for copy in first:
            copy.wait_send()
        for copy in second:
            copy.wait_send()
        for t in range(count - 1):
            source = lax.rem(me + count - 1 - t, count)
            theirs = pl.ds(pl.multiple_of(source * piece, piece), piece)
            remote(
                o_ref.at[theirs], o_ref.at[theirs], send.at[1, t], recv.at[1, t], devices[t]
            ).wait_recv()
        for copy in carried:
            copy.wait()

    total, *outs = pl.pallas_call(
        kernel,
        out_shape=[jax.ShapeDtypeStruct((rows, width), jnp.bfloat16)]
        + [
            jax.ShapeDtypeStruct((many,) + cut(a.shape, dim), a.dtype)
            for (a, _, dim), many in zip(riders, extra)
        ],
        in_specs=[VMEM] + [ANY] * size,
        out_specs=[VMEM] + [ANY] * size,
        scratch_shapes=[
            pltpu.VMEM((count - 1, piece, width), jnp.bfloat16),
            pltpu.SemaphoreType.DMA((2, count - 1)),
            pltpu.SemaphoreType.DMA((2, count - 1)),
        ]
        + [pltpu.SemaphoreType.DMA((many,)) for many in extra for _ in range(2)],
        compiler_params=pltpu.CompilerParams(collective_id=ident, has_side_effects=True),
        name="total_mp",
    )(values, *[a for a, _, _ in riders])
    return total, [gathered(o, *rider) for o, rider in zip(outs, riders)]


def spread(arrays, kind, ident, dim=0):
    me, count = rank_of(kind)
    size = len(arrays)

    def kernel(*refs):
        ins, outs, (send, recv) = refs[:size], refs[size : 2 * size], refs[2 * size :]
        rank, _ = rank_of(kind)
        devices = [device_of(kind, lax.rem(rank + t, count)) for t in range(1, count)]
        greet(devices)
        copies = []
        for t in range(count - 1):
            for i in range(size):
                copy = remote(ins[i], pick(outs[i], rank, dim), send.at[i, t], recv.at[i, t], devices[t])
                copy.start()
                copies.append(copy)
        for copy in copies:
            copy.wait_send()
        for t in range(count - 1):
            source = lax.rem(rank + count - 1 - t, count)
            for i in range(size):
                remote(
                    ins[i], pick(outs[i], source, dim), send.at[i, t], recv.at[i, t], devices[t]
                ).wait_recv()

    outs = pl.pallas_call(
        kernel,
        out_shape=[
            jax.ShapeDtypeStruct(a.shape[:dim] + (count,) + a.shape[dim:], a.dtype) for a in arrays
        ],
        in_specs=[ANY] * size,
        out_specs=[ANY] * size,
        scratch_shapes=[pltpu.SemaphoreType.DMA((size, count - 1))] * 2,
        compiler_params=pltpu.CompilerParams(collective_id=ident, has_side_effects=True),
        name="spread_" + kind,
    )(*arrays)
    return [lax.dynamic_update_index_in_dim(o, a, me, dim) for o, a in zip(outs, arrays)]


def spread_all(arrays, ident):
    me, total = rank_of("flat")
    size = len(arrays)
    chips = total // 2

    def kernel(*refs):
        ins, outs, (send, recv, send2, recv2) = refs[:size], refs[size : 2 * size], refs[2 * size :]
        chip, _ = rank_of("chip")
        core, _ = rank_of("core")
        rank = chip * 2 + core
        other = chip * 2 + 1 - core
        devices = [device_of("chip", lax.rem(chip + t, chips)) for t in range(1, chips)]
        sibling = device_of("core", 1 - core)
        greet(devices + [sibling])
        sent = []
        for i in range(size):
            for t in range(chips - 1):
                copy = remote(ins[i], outs[i].at[rank], send.at[i, t], recv.at[i, t], devices[t])
                copy.start()
                sent.append(copy)
        for i in range(size):
            copy = remote(
                ins[i], outs[i].at[rank], send2.at[i, 0], recv2.at[i, 0], sibling
            )
            copy.start()
            sent.append(copy)
        for i in range(size):
            for t in range(chips - 1):
                source = lax.rem(chip + chips - 1 - t, chips) * 2 + core
                remote(
                    ins[i], outs[i].at[source], send.at[i, t], recv.at[i, t], devices[t]
                ).wait_recv()
                copy = remote(
                    outs[i].at[source], outs[i].at[source],
                    send2.at[i, t + 1], recv2.at[i, t + 1], sibling,
                )
                copy.start()
                sent.append(copy)
        for copy in sent:
            copy.wait_send()
        for i in range(size):
            remote(
                ins[i], outs[i].at[other], send2.at[i, 0], recv2.at[i, 0], sibling
            ).wait_recv()
            for t in range(chips - 1):
                source = lax.rem(chip + chips - 1 - t, chips) * 2 + 1 - core
                remote(
                    ins[i], outs[i].at[source],
                    send2.at[i, t + 1], recv2.at[i, t + 1], sibling,
                ).wait_recv()

    outs = pl.pallas_call(
        kernel,
        out_shape=[jax.ShapeDtypeStruct((total,) + a.shape, a.dtype) for a in arrays],
        in_specs=[ANY] * size,
        out_specs=[ANY] * size,
        scratch_shapes=[pltpu.SemaphoreType.DMA((size, chips - 1))] * 2
        + [pltpu.SemaphoreType.DMA((size, chips))] * 2,
        compiler_params=pltpu.CompilerParams(collective_id=ident, has_side_effects=True),
        name="spread_all",
    )(*arrays)
    return [lax.dynamic_update_index_in_dim(o, a, me, 0) for o, a in zip(outs, arrays)]


def trade(arrays, kind, ident, dim=0):
    _, count = rank_of(kind)
    size = len(arrays)

    def kernel(*refs):
        ins, outs, (send, recv) = refs[:size], refs[size : 2 * size], refs[2 * size :]
        rank, _ = rank_of(kind)
        ranks = [lax.rem(rank + t, count) for t in range(1, count)]
        devices = [device_of(kind, peer) for peer in ranks]
        greet(devices)
        copies = []
        for t in range(count - 1):
            for i in range(size):
                copy = remote(
                    pick(ins[i], ranks[t], dim), outs[i].at[t], send.at[i, t], recv.at[i, t], devices[t]
                )
                copy.start()
                copies.append(copy)
        for copy in copies:
            copy.wait()

    outs = pl.pallas_call(
        kernel,
        out_shape=[jax.ShapeDtypeStruct((count - 1,) + cut(a.shape, dim), a.dtype) for a in arrays],
        in_specs=[ANY] * size,
        out_specs=[ANY] * size,
        scratch_shapes=[pltpu.SemaphoreType.DMA((size, count - 1))] * 2,
        compiler_params=pltpu.CompilerParams(collective_id=ident, has_side_effects=True),
        name="trade_" + kind,
    )(*arrays)
    return [gathered(o, a, kind, dim) for o, a in zip(outs, arrays)]


def block_mask(q_pos, q_seg, key_seg, start, block):
    k_pos = start + jnp.arange(block, dtype=jnp.int32)
    seg_keys = lax.dynamic_slice_in_dim(key_seg, start, block, 1)
    mask = (k_pos[None, None, :] <= q_pos[None, :, None]) & (
        seg_keys[:, None, :] == q_seg[:, :, None]
    )
    return mask[:, None]


def block_scores(query, keys, q_pos, start, block, slope, scale):
    k_pos = start + jnp.arange(block, dtype=jnp.int32)
    dist = (q_pos[:, None] - k_pos[None, :]).astype(jnp.float32)
    score = jnp.einsum("sqhd,skhd->shqk", query, keys, preferred_element_type=jnp.float32)
    return score * scale - slope[None, :, None, None] * dist[None, None]


def attend_forward(query, keys, values, q_pos, q_seg, key_seg, slope):
    seqs, rows, heads, width = query.shape
    length = keys.shape[1]
    block = min(512, length)
    scale = 1.0 / math.sqrt(width)

    def step(carry, index):
        start = index * block
        mask = block_mask(q_pos, q_seg, key_seg, start, block)

        def work(state):
            acc, total = state
            key_part = lax.dynamic_slice_in_dim(keys, start, block, 1)
            value_part = lax.dynamic_slice_in_dim(values, start, block, 1)
            score = block_scores(query, key_part, q_pos, start, block, slope, scale)
            expo = jnp.where(mask, jnp.exp(jnp.where(mask, score, 0.0)), 0.0)
            acc = acc + jnp.einsum(
                "shqk,skhd->sqhd",
                expo.astype(jnp.bfloat16),
                value_part,
                preferred_element_type=jnp.float32,
            )
            return (acc, total + jnp.sum(expo, -1))

        if length == block:
            return (work(carry), None)
        return (lax.cond(jnp.any(mask), work, lambda state: state, carry), None)

    init = (jnp.zeros(query.shape, jnp.float32), jnp.zeros((seqs, heads, rows), jnp.float32))
    if length == block:
        (acc, total), _ = step(init, 0)
    else:
        (acc, total), _ = lax.scan(step, init, jnp.arange(length // block, dtype=jnp.int32))
    ctx = (acc / jnp.transpose(total, (0, 2, 1))[..., None]).astype(jnp.bfloat16)
    return (ctx, jnp.log(total))


def attend_backward(query, keys, values, q_pos, q_seg, key_seg, slope, ctx, lse, dctx):
    seqs, rows, heads, width = query.shape
    length = keys.shape[1]
    block = min(512, length)
    scale = 1.0 / math.sqrt(width)
    delta = jnp.transpose(
        jnp.sum(dctx.astype(jnp.float32) * ctx.astype(jnp.float32), -1), (0, 2, 1)
    )

    def step(carry, index):
        start = index * block
        mask = block_mask(q_pos, q_seg, key_seg, start, block)

        def work(state):
            grad_q, grad_keys, grad_values = state
            key_part = lax.dynamic_slice_in_dim(keys, start, block, 1)
            value_part = lax.dynamic_slice_in_dim(values, start, block, 1)
            score = block_scores(query, key_part, q_pos, start, block, slope, scale)
            prob = jnp.where(mask, jnp.exp(jnp.where(mask, score - lse[..., None], 0.0)), 0.0)
            grad_v = jnp.einsum(
                "shqk,sqhd->skhd",
                prob.astype(jnp.bfloat16),
                dctx,
                preferred_element_type=jnp.float32,
            )
            grad_p = jnp.einsum(
                "sqhd,skhd->shqk", dctx, value_part, preferred_element_type=jnp.float32
            )
            grad_s = (prob * (grad_p - delta[..., None])).astype(jnp.bfloat16)
            grad_q = (
                grad_q
                + jnp.einsum(
                    "shqk,skhd->sqhd", grad_s, key_part, preferred_element_type=jnp.float32
                )
                * scale
            )
            grad_k = (
                jnp.einsum("shqk,sqhd->skhd", grad_s, query, preferred_element_type=jnp.float32)
                * scale
            )
            if length == block:
                return (grad_q, grad_k, grad_v)
            return (
                grad_q,
                lax.dynamic_update_slice_in_dim(grad_keys, grad_k, start, 1),
                lax.dynamic_update_slice_in_dim(grad_values, grad_v, start, 1),
            )

        if length == block:
            return (work(carry), None)
        return (lax.cond(jnp.any(mask), work, lambda state: state, carry), None)

    init = (
        jnp.zeros(query.shape, jnp.float32),
        jnp.zeros(keys.shape, jnp.float32),
        jnp.zeros(keys.shape, jnp.float32),
    )
    if length == block:
        grads, _ = step(init, 0)
    else:
        grads, _ = lax.scan(step, init, jnp.arange(length // block, dtype=jnp.int32))
    return grads


def per_device(hidden_in, segment_ids, gains, biases, w_qkv, w_out_t, w_up, w_down_t, grad_out):
    seqs, rows, width = hidden_in.shape
    layers = w_qkv.shape[0]
    cols = w_qkv.shape[3]
    ff_cols = w_up.shape[2]
    heads = cols // HEAD
    mp_count = lax.axis_size("mp")
    mp_index = lax.axis_index("mp")
    layers_rows = gains.shape[0] * gains.shape[1]
    bias_count = biases.shape[0] * biases.shape[1]
    part = gains.shape[2]
    vectors = jnp.concatenate(
        [gains.reshape(layers_rows, part), biases.reshape(bias_count, part)], 0
    )
    (vectors,) = spread([vectors], "mp", 1)
    first = spread_all(
        [
            w_qkv[0].reshape(-1, 3 * cols),
            w_out_t[0],
            w_up[0],
            w_down_t[0],
            vectors.reshape(-1, part),
            segment_ids,
        ],
        2,
    )
    owners = first[4].shape[0]
    vectors = jnp.transpose(
        first[4].reshape(owners, mp_count, layers_rows + bias_count, part), (2, 0, 1, 3)
    ).reshape(layers_rows + bias_count, width)
    all_gains = vectors[:layers_rows].reshape(gains.shape[:2] + (width,))
    all_biases = vectors[layers_rows:].reshape(biases.shape[:2] + (width,))
    ctx_count = lax.axis_size("ctx")
    key_seg = lax.dynamic_slice_in_dim(
        first[5], lax.axis_index("batch") * ctx_count, ctx_count, 0
    )
    key_seg = jnp.transpose(key_seg, (1, 0, 2)).reshape(seqs, ctx_count * rows)
    first_weights = (
        first[0].reshape(width, 3, cols),
        first[1].reshape(width, cols),
        first[2].reshape(width, ff_cols),
        first[3].reshape(width, ff_cols),
    )

    def ride_mp(values, riders=(), ident=0):
        flat = values.reshape(seqs * rows, width).astype(jnp.bfloat16)
        total, sums = total_mp(flat, riders, ident)
        return total.reshape(values.shape).astype(jnp.float32), sums

    def sum_mp(values):
        return ride_mp(values)[0]

    def core_riders(arrays):
        return [
            (
                a.astype(jnp.bfloat16).reshape(owners // 2, 2, width // owners, a.shape[1]),
                "core",
                1,
            )
            for a in arrays
        ]

    def chip_riders(arrays):
        return [(a.astype(jnp.bfloat16), "chip", 0) for a in arrays]

    q_pos = lax.axis_index("ctx") * rows + jnp.arange(rows, dtype=jnp.int32)
    head_ids = (mp_index * heads + jnp.arange(heads, dtype=jnp.int32)).astype(jnp.float32)
    slope = jnp.exp2(-8.0 * (head_ids + 1.0) / HEADS)
    own = (jnp.arange(width, dtype=jnp.int32) // cols == mp_index).astype(jnp.float32)
    full_ff = ff_cols * mp_count

    def place(values, offset, total):
        return lax.dynamic_update_slice_in_dim(jnp.zeros((total,), jnp.float32), values, offset, 0)

    def unpack(layer):
        vec = all_biases[layer]
        query_bias = lax.dynamic_slice_in_dim(vec[2], mp_index * cols, cols, 0)
        value_bias = lax.dynamic_slice_in_dim(vec[3], mp_index * cols, cols, 0)
        up_projection_bias = lax.dynamic_slice_in_dim(
            vec[6:].reshape(-1), mp_index * ff_cols, ff_cols, 0
        )
        return (vec, query_bias, value_bias, up_projection_bias)

    def forward_layer(layer, state, weights):
        query_weight, w_o, up_weight, w_d = weights
        vec, query_bias, value_bias, up_projection_bias = unpack(layer)
        normed1, _ = norm_parts(state)
        first_activation = (normed1 * all_gains[layer, 0] + vec[0]).astype(jnp.bfloat16)
        query_key_value = jnp.einsum(
            "bph,hue->bpue", first_activation, query_weight, preferred_element_type=jnp.float32
        )
        shift = jnp.stack([query_bias, jnp.zeros_like(query_bias), value_bias])
        qkv_bf = (query_key_value + shift).astype(jnp.bfloat16)
        kv_all = [
            item.reshape(seqs, -1, heads, HEAD)
            for item in spread([qkv_bf[:, :, 1], qkv_bf[:, :, 2]], "ctx", 3, 1)
        ]
        query = qkv_bf[:, :, 0].reshape(seqs, rows, heads, HEAD)
        ctx, lse = attend_forward(query, *kv_all, q_pos, segment_ids, key_seg, slope)
        ctx_flat = ctx.reshape(seqs, rows, cols)
        part = jnp.einsum("slc,oc->slo", ctx_flat, w_o, preferred_element_type=jnp.float32)
        mid = state + sum_mp(part) + vec[4]
        normed2, _ = norm_parts(mid)
        second_activation = (normed2 * all_gains[layer, 1] + vec[1]).astype(jnp.bfloat16)
        up_projected = (
            jnp.einsum(
                "nhz,zb->nhb", second_activation, up_weight, preferred_element_type=jnp.float32
            )
            + up_projection_bias
        )
        act, _ = gelu_parts(up_projected)
        act_bf = act.astype(jnp.bfloat16)
        down = jnp.einsum("slf,of->slo", act_bf, w_d, preferred_element_type=jnp.float32)
        result = mid + sum_mp(down) + vec[5]
        return (
            result,
            (
                state,
                first_activation,
                qkv_bf,
                kv_all,
                ctx_flat,
                lse,
                mid,
                second_activation,
                up_projected,
                act_bf,
            ),
        )

    state = hidden_in.astype(jnp.float32)
    saves = []
    for layer in range(layers):
        weights = first_weights if layer == 0 else (
            lax.all_gather(w_qkv[layer], ("batch", "ctx"), axis=0, tiled=True),
            lax.all_gather(w_out_t[layer], ("batch", "ctx"), axis=0, tiled=True),
            lax.all_gather(w_up[layer], ("batch", "ctx"), axis=0, tiled=True),
            lax.all_gather(w_down_t[layer], ("batch", "ctx"), axis=0, tiled=True),
        )
        state, saved = forward_layer(layer, state, weights)
        saves.append((weights, saved))
    output = state.astype(jnp.bfloat16)
    grad = grad_out.astype(jnp.float32)
    gain_rows = [None] * layers
    bias_rows = [None] * layers
    finished = [None] * layers
    pending = []
    for layer in reversed(range(layers)):
        kept_weights, saved = saves[layer]
        (
            x_in,
            first_activation,
            qkv_bf,
            kv_kept,
            ctx_flat,
            lse,
            mid,
            second_activation,
            up_projected,
            act_bf,
        ) = saved
        query_weight, w_o, up_weight, w_d = kept_weights
        kv_all = kv_kept
        gain1 = all_gains[layer, 0]
        gain2 = all_gains[layer, 1]
        grad_bf = grad.astype(jnp.bfloat16)
        grad_bd = jnp.sum(grad, (0, 1))
        grad_wd = jnp.einsum("slo,slf->of", grad_bf, act_bf, preferred_element_type=jnp.float32)
        dact = jnp.einsum("slo,of->slf", grad_bf, w_d, preferred_element_type=jnp.float32)
        _, bend = gelu_parts(up_projected)
        dup = dact * gelu_slope(up_projected, bend)
        grad_bu = jnp.sum(dup, (0, 1))
        up_gradient_half_precision = dup.astype(jnp.bfloat16)
        up_weight_gradient = jnp.einsum(
            "qwi,qwn->in",
            second_activation,
            up_gradient_half_precision,
            preferred_element_type=jnp.float32,
        )
        da2 = jnp.einsum(
            "cju,xu->cjx",
            up_gradient_half_precision,
            up_weight,
            preferred_element_type=jnp.float32,
        )
        late = chip_riders(pending)
        da2, sums = ride_mp(
            da2, core_riders([up_weight_gradient, grad_wd]) + late, 6 if late else 7
        )
        unit_halves = sums[:2]
        if late:
            finished[layer + 1] += sums[2:]
        normed2, inverse2 = norm_parts(mid)
        grad_g2 = jnp.sum(da2 * normed2, (0, 1))
        grad_b2 = jnp.sum(da2, (0, 1))
        gx2 = grad + norm_back(da2, normed2, inverse2, gain2)
        grad_bo = jnp.sum(gx2, (0, 1))
        gx2_bf = gx2.astype(jnp.bfloat16)
        grad_wo = jnp.einsum("slo,slc->oc", gx2_bf, ctx_flat, preferred_element_type=jnp.float32)
        dctx = jnp.einsum("slo,oc->slc", gx2_bf, w_o, preferred_element_type=jnp.float32).astype(
            jnp.bfloat16
        )
        query = qkv_bf[:, :, 0].reshape(seqs, rows, heads, HEAD)
        ctx_heads = ctx_flat.reshape(seqs, rows, heads, HEAD)
        dctx_heads = dctx.reshape(seqs, rows, heads, HEAD)
        grad_q, *grad_kv_terms = attend_backward(
            query, *kv_all, q_pos, segment_ids, key_seg, slope, ctx_heads, lse, dctx_heads
        )
        kv_terms = [
            item.astype(jnp.bfloat16).reshape(seqs, ctx_count, rows, cols)
            for item in grad_kv_terms
        ]
        grad_kv = jnp.stack(trade(kv_terms, "ctx", 4, 1), 2)
        grad_qf = grad_q.reshape(seqs, rows, cols)
        grad_bq = jnp.sum(grad_qf, (0, 1))
        value_bias_gradient = jnp.sum(grad_kv[:, :, 1], (0, 1))
        packed_projection_gradient = jnp.concatenate([grad_qf[:, :, None], grad_kv], 2).astype(
            jnp.bfloat16
        )
        query_weight_gradient = jnp.einsum(
            "ebz,ebpy->zpy",
            first_activation,
            packed_projection_gradient,
            preferred_element_type=jnp.float32,
        )
        da1 = jnp.einsum(
            "aewu,vwu->aev",
            packed_projection_gradient,
            query_weight,
            preferred_element_type=jnp.float32,
        )
        da1, sums = ride_mp(
            da1,
            core_riders([query_weight_gradient.reshape(width, 3 * cols), grad_wo])
            + chip_riders(unit_halves),
            8,
        )
        pending = sums[:2]
        finished[layer] = sums[2:]
        normed1, inverse1 = norm_parts(x_in)
        grad_g1 = jnp.sum(da1 * normed1, (0, 1))
        grad_b1 = jnp.sum(da1, (0, 1))
        grad = gx2 + norm_back(da1, normed1, inverse1, gain1)
        gain_rows[layer] = jnp.stack([grad_g1 * own, grad_g2 * own])
        head_rows = jnp.stack(
            [
                grad_b1 * own,
                grad_b2 * own,
                place(grad_bq, mp_index * cols, width),
                place(value_bias_gradient, mp_index * cols, width),
                grad_bo * own,
                grad_bd * own,
            ]
        )
        unit_rows = place(grad_bu, mp_index * ff_cols, full_ff).reshape(full_ff // width, width)
        bias_rows[layer] = jnp.concatenate([head_rows, unit_rows], 0)
    row_count = layers_rows + bias_count
    terms = jnp.concatenate(
        [
            jnp.stack(gain_rows).reshape(layers_rows, width),
            jnp.stack(bias_rows).reshape(bias_count, width),
        ],
        0,
    ).reshape(row_count, owners, mp_count, part)
    terms = jnp.transpose(terms, (2, 0, 1, 3)).reshape(mp_count, row_count, owners * part)
    (terms,) = trade([terms], "mp", 5)
    terms = jnp.transpose(terms.reshape(row_count, owners, part), (1, 0, 2))
    (terms,) = trade([terms.reshape(owners // 2, 2, row_count, part)], "core", 9, 1)
    *tail, terms = trade([item.astype(jnp.bfloat16) for item in pending] + [terms], "chip", 10)
    finished[0] += tail
    grad_gains = terms[:layers_rows].reshape(gains.shape)
    grad_biases = terms[layers_rows:].reshape(biases.shape)
    grad_qkv = jnp.stack([item[2] for item in finished]).reshape(w_qkv.shape)
    grad_attn_out = jnp.stack([item[3] for item in finished])
    grad_up = jnp.stack([item[0] for item in finished])
    grad_down = jnp.stack([item[1] for item in finished])
    return (
        output,
        grad.astype(jnp.bfloat16),
        grad_gains,
        grad_biases,
        grad_qkv,
        grad_attn_out,
        grad_up,
        grad_down,
    )


def solution(mesh):
    in_specs = (
        P("batch", "ctx", None),
        P("batch", "ctx"),
        P(None, None, ("batch", "ctx", "mp")),
        P(None, None, ("batch", "ctx", "mp")),
        P(None, ("batch", "ctx"), None, "mp"),
        P(None, ("batch", "ctx"), "mp"),
        P(None, ("batch", "ctx"), "mp"),
        P(None, ("batch", "ctx"), "mp"),
        P("batch", "ctx", None),
    )
    out_specs = (
        P("batch", "ctx", None),
        P("batch", "ctx", None),
        P(None, None, ("batch", "ctx", "mp")),
        P(None, None, ("batch", "ctx", "mp")),
        P(None, ("batch", "ctx"), None, "mp"),
        P(None, ("batch", "ctx"), "mp"),
        P(None, ("batch", "ctx"), "mp"),
        P(None, ("batch", "ctx"), "mp"),
    )
    return jax.shard_map(
        per_device, mesh=mesh, in_specs=in_specs, out_specs=out_specs, check_vma=False
    )
```
